512 devices in a mesh: group: 4 (over x), shard: 128 (over y, z, core).
Axes of the slice: x: 4, y: 4, z: 16, core: 2. Of those that a mesh axis runs over, the one named last changes fastest.
Arguments:
- amplitudes: float32 [524288, 128], P(('group', 'shard')), may hold values from -6 to 6
- orbit_index: int32 [524288, 128], P(('group', 'shard')), may hold values from 0 to 5
- requests: int32 [512, 512, 2], P(('group', 'shard')), may hold values from 0 to 1024, as said below
- targets: int32 [512, 512, 2], P(('group', 'shard')), may hold values from 0 to 1023
Outputs:
- image: float32 [524288, 128], P(('group', 'shard'))
The draws below stay inside these ranges and needn't reach their ends.
Inputs may be any that keep to these rules, and one draw needn't show every extreme that they name: `requests`: each value is an owner's local block number below 1024, or 1024 for an empty slot; in every list from one requester to one owner the used slots come first; every draw has owners whose lists from every requester are full (2 blocks).
All inputs are finite; a program needn't handle non-finite values.
Results may differ from the reference program's by a relative error of at most 0.0003.
Values sent between devices are 32-bit elements; how exact they have to be, the bound alone decides.
No kernel may reach another device: no remote copies, remote signals or barrier semaphores. Data moves between devices by JAX's collectives and lax.ppermute only.
A program may use at most 64 MiB of HBM per device.

```python
import jax
import jax.numpy as jnp
from jax import lax

NB = 1024
BLK = 128
CAP = 2
RANKS = 512
TOTAL_BLOCKS = 524288


def draw_requests(key, part):
    first, second, third = jax.random.split(key, 3)
    counts = jax.random.randint(first, (RANKS, RANKS), max(1, CAP // 2), CAP + 1)
    popular = jax.random.randint(second, (4,), 0, RANKS)
    is_popular = jnp.any(jnp.arange(RANKS)[:, None] == popular[None, :], axis=1)
    counts = jnp.where(is_popular[None, :], CAP, counts)
    numbers = jax.random.randint(third, (RANKS, RANKS, CAP), 0, NB)
    slots = jnp.arange(CAP)
    return jnp.where(slots[None, None, :] < counts[:, :, None], numbers, NB).astype(jnp.int32)


def place_ends(array, stream_key, smallest, top_value):
    shape = array.shape
    spot = [jax.random.randint(jax.random.fold_in(stream_key, axis), (), 0, shape[axis]) for axis in range(len(shape))]
    array = array.at[tuple(spot)].set(smallest)
    longest = shape.index(max(shape))
    spot[longest] = (spot[longest] + 1) % shape[longest]
    return array.at[tuple(spot)].set(top_value)


def block_levels(key, dims, cuts, least, high):
    loudness = 1.0
    for dim, parts in cuts:
        heights = jax.random.uniform(jax.random.fold_in(jax.random.fold_in(key, 6), dim), (parts,), jnp.float32, least / len(cuts), high / len(cuts))
        loudness = loudness * jnp.repeat(jnp.exp(heights), dims[dim] // parts).reshape((-1,) + (1,) * (len(dims) - 1 - dim))
    return loudness


def centred(rng, extent, width, bound, shards=(), held_as=jnp.bfloat16):
    factor_of = block_levels(rng, extent, shards, -0.22, 0.18) if shards else 1.0
    array = jax.random.normal(rng, extent, jnp.float32) * width * factor_of
    return jnp.minimum(jnp.maximum(array, -bound), bound).astype(held_as)


def setup_inputs(seed: int = 0) -> dict:
    key_list = jax.random.split(jax.random.key(seed), 5)
    return {
        "amplitudes": centred(key_list[0], (TOTAL_BLOCKS, BLK), 1.0, 6.0, ((0, 512),), jnp.float32),
        "orbit_index": place_ends(jax.random.randint(key_list[1], (TOTAL_BLOCKS, BLK), 0, 6), jax.random.fold_in(key_list[1], 1), 0, 5).astype(jnp.int32),
        "requests": draw_requests(jax.random.fold_in(key_list[4], 71), 0),
        "targets": place_ends(jax.random.randint(key_list[3], (RANKS, RANKS, CAP), 0, NB), jax.random.fold_in(key_list[3], 1), 0, NB - 1).astype(jnp.int32),
    }


def reference(amplitudes, orbit_index, requests, targets):
    factor = jnp.sqrt(96.0 * jnp.exp2(-orbit_index.astype(amplitudes.dtype)))
    weighted = amplitudes * factor
    total = weighted.shape[0]
    lanes = weighted.shape[1]
    padded = jnp.concatenate([weighted, jnp.zeros((1, lanes), weighted.dtype)], axis=0)
    owners = jnp.arange(RANKS, dtype=jnp.int32)

    def visit(totals, requester):
        wanted = requests[requester]
        valid = wanted < NB
        global_rows = jnp.where(valid, owners[:, None] * NB + wanted, total).astype(jnp.int32).reshape(-1)
        places = (requester * NB + targets[requester]).astype(jnp.int32).reshape(-1)
        fetched = padded[global_rows]
        totals = totals.at[places].add(fetched)
        totals = totals.at[global_rows].add(weighted[places])
        return (totals, None)
    start = jnp.zeros((total + 1, lanes), weighted.dtype)
    totals, unused = lax.scan(visit, start, jnp.arange(RANKS, dtype=jnp.int32))
    return totals[:total] / factor
```

```python
import jax
import jax.numpy as jnp
from jax import lax
from jax.experimental import pallas as pl
from jax.experimental.pallas import tpu as pltpu
from jax.sharding import Mesh
from jax.sharding import PartitionSpec as P

AXES = ("x", "y", "z", "c")
PEERS = ("z", "x", "y", "c")
PLANE = ("x", "y", "c")


def orbit_factor(orbit):
    return jnp.sqrt(96.0 * jnp.exp2(-orbit.astype(jnp.float32)))


def two_parts(values):
    high = values.astype(jnp.bfloat16)
    low = (values - high.astype(jnp.float32)).astype(jnp.bfloat16)
    return jnp.concatenate([high, low], axis=1)


def halves_added(product):
    columns = product.shape[1] // 2
    return product[:, :columns] + product[:, columns:]


def weigh_kernel(amplitudes_ref, orbit_ref, table_ref):
    table_ref[...] = two_parts(amplitudes_ref[...] * orbit_factor(orbit_ref[...]))


def weigh(amplitudes, orbit):
    blocks, columns = amplitudes.shape
    return pl.pallas_call(
        weigh_kernel,
        out_shape=jax.ShapeDtypeStruct((blocks, 2 * columns), jnp.bfloat16),
        cost_estimate=pl.CostEstimate(
            flops=blocks * columns * 8,
            bytes_accessed=blocks * columns * 12,
            transcendentals=blocks * columns,
        ),
        name="weigh",
    )(amplitudes, orbit)


def pick_kernel(index_ref, table_ref, rows_ref, chosen_ref):
    groups, lanes = index_ref.shape
    blocks = table_ref.shape[0]
    lane = lax.broadcasted_iota(jnp.int32, (lanes, lanes), 1)
    for group in range(groups):
        numbers = jnp.broadcast_to(index_ref[group : group + 1, :], (lanes, lanes)).T
        for start in range(0, blocks, lanes):
            hit = numbers == lane + start
            chosen_ref[group * lanes : (group + 1) * lanes, start : start + lanes] = (
                jnp.where(hit, 1.0, 0.0).astype(jnp.bfloat16)
            )
    product = jnp.dot(
        chosen_ref[...], table_ref[...], preferred_element_type=jnp.float32
    )
    rows_ref[...] = halves_added(product)


def pick(index, table):
    rows = index.size
    blocks, width = table.shape
    return pl.pallas_call(
        pick_kernel,
        out_shape=jax.ShapeDtypeStruct((rows, width // 2), jnp.float32),
        scratch_shapes=[pltpu.VMEM((rows, blocks), jnp.bfloat16)],
        cost_estimate=pl.CostEstimate(
            flops=2 * rows * blocks * width,
            bytes_accessed=rows * width * 2 + blocks * width * 2,
            transcendentals=0,
        ),
        name="pick",
    )(index, table)


def gather_up_kernel(index_ref, rows_ref, orbit_ref, out_ref, chosen_ref):
    groups, lanes = index_ref.shape
    blocks = out_ref.shape[0]
    block = lax.broadcasted_iota(jnp.int32, (blocks, lanes), 0)
    for group in range(groups):
        hit = block == index_ref[group : group + 1, :]
        chosen_ref[:, group * lanes : (group + 1) * lanes] = jnp.where(
            hit, 1.0, 0.0
        ).astype(jnp.bfloat16)
    product = jnp.dot(
        chosen_ref[...], two_parts(rows_ref[...]), preferred_element_type=jnp.float32
    )
    out_ref[...] = halves_added(product) / orbit_factor(orbit_ref[...])


def gather_up(index, rows, orbit):
    blocks, columns = orbit.shape
    count = rows.shape[0]
    return pl.pallas_call(
        gather_up_kernel,
        out_shape=jax.ShapeDtypeStruct((blocks, columns), jnp.float32),
        scratch_shapes=[pltpu.VMEM((blocks, count), jnp.bfloat16)],
        cost_estimate=pl.CostEstimate(
            flops=4 * count * blocks * columns,
            bytes_accessed=(count + 2 * blocks) * columns * 4,
            transcendentals=blocks * columns,
        ),
        name="gather_up",
    )(index, rows, orbit)


def per_device(amplitudes, orbit_index, requests, targets):
    columns = amplitudes.shape[1]
    nx, ny, nz, nc = (lax.axis_size(a) for a in AXES)
    plane = nx * ny * nc
    slots = requests.shape[-1]
    asked = requests.reshape(nx, ny, nz, nc, slots).transpose(0, 1, 3, 4, 2)
    asked = asked.reshape(plane, slots, nz)
    asked = lax.all_to_all(asked, PLANE, split_axis=0, concat_axis=0, tiled=True)
    asked = asked.transpose(2, 0, 1).reshape(nz, 1, plane * slots)
    asked = lax.all_to_all(asked, "z", split_axis=0, concat_axis=0, tiled=True)
    incoming = asked.reshape(nz, plane, slots)
    places = targets.reshape(nx, ny, nz, nc, slots).transpose(2, 0, 1, 3, 4)
    places = places.reshape(nz, plane, slots)
    table = weigh(amplitudes, orbit_index)
    outgoing_index = jnp.concatenate([places, incoming], axis=-1).reshape(-1, 128)
    landing_index = jnp.concatenate([incoming, places], axis=-1).reshape(-1, 128)
    outgoing = pick(outgoing_index, table)
    arrived = lax.all_to_all(
        outgoing.reshape(nz * plane, 2 * slots, columns),
        PEERS,
        split_axis=0,
        concat_axis=0,
        tiled=True,
    )
    return gather_up(landing_index, arrived.reshape(-1, columns), orbit_index)


def solution(mesh):
    groups, shards = mesh.devices.shape
    devices = mesh.devices.reshape(groups, 4, shards // 8, 2)
    split = P(AXES)
    return jax.shard_map(
        per_device,
        mesh=Mesh(devices, AXES),
        in_specs=(split, split, split, split),
        out_specs=split,
        check_vma=False,
    )
```

```python
import jax
import jax.numpy as jnp
from jax import lax
from jax.experimental import pallas as pl
from jax.experimental.pallas import tpu as pltpu
from jax.sharding import Mesh
from jax.sharding import PartitionSpec as P

AXES = ("x", "y", "z", "c")
PEERS = ("z", "x", "y", "c")
PLANE = ("x", "y", "c")
IN_VMEM = pl.BlockSpec(memory_space=pltpu.VMEM)
MIB = 2**20
STEP = 8


def orbit_factor(orbit):
    return jnp.sqrt(96.0 * jnp.exp2(-orbit.astype(jnp.float32)))


def two_parts(values):
    high = values.astype(jnp.bfloat16)
    low = (values - high.astype(jnp.float32)).astype(jnp.bfloat16)
    return jnp.concatenate([high, low], axis=1)


def halves_added(product):
    columns = product.shape[1] // 2
    return product[:, :columns] + product[:, columns:]


def ones_where(hit):
    return jnp.where(hit, 1.0, 0.0).astype(jnp.bfloat16)


def picked(numbers, table, slots, step):
    lines, width = numbers.shape
    blocks = table.shape[0]
    columns = numbers.T
    block = lax.broadcasted_iota(jnp.int32, (width, blocks), 1)
    for slot in range(slots):
        for first in range(0, lines // slots, step):
            chosen = [
                ones_where(columns[:, row : row + 1] == block)
                for row in range(first * slots + slot, (first + step) * slots + slot, slots)
            ]
            product = jnp.dot(
                jnp.concatenate(chosen, axis=0), table, preferred_element_type=jnp.float32
            )
            yield slot, first * width, halves_added(product)


def own_kernel(slots, amplitudes_ref, orbit_ref, places_ref, table_ref, own_ref):
    table_ref[...] = two_parts(amplitudes_ref[...] * orbit_factor(orbit_ref[...]))
    peers = own_ref.shape[0] // slots
    for slot, first, rows in picked(places_ref[...], table_ref[...], slots, STEP):
        start = slot * peers + first
        own_ref[start : start + rows.shape[0], :] = rows


def own_rows(amplitudes, orbit, places, slots):
    blocks, columns = amplitudes.shape
    rows = places.size
    return pl.pallas_call(
        lambda *refs: own_kernel(slots, *refs),
        out_shape=(
            jax.ShapeDtypeStruct((blocks, 2 * columns), jnp.bfloat16),
            jax.ShapeDtypeStruct((rows, columns), jnp.float32),
        ),
        in_specs=[IN_VMEM] * 3,
        out_specs=(IN_VMEM, IN_VMEM),
        compiler_params=pltpu.CompilerParams(vmem_limit_bytes=16 * MIB),
        cost_estimate=pl.CostEstimate(
            flops=4 * rows * blocks * columns,
            bytes_accessed=20 * blocks * columns,
            transcendentals=blocks * columns,
        ),
        name="own_rows",
    )(amplitudes, orbit, places)


def serve_kernel(slots, wanted_ref, table_ref, own_ref, out_ref):
    peers = own_ref.shape[0] // slots
    for slot in range(slots):
        part = slice(slot * peers, (slot + 1) * peers)
        out_ref[pl.ds(slot, peers, stride=2 * slots), :] = own_ref[part, :]
    for slot, first, rows in picked(wanted_ref[...], table_ref[...], slots, STEP):
        start = first * 2 * slots + slots + slot
        out_ref[pl.ds(start, rows.shape[0], stride=2 * slots), :] = rows


def serve(wanted, table, own, slots):
    rows, columns = own.shape
    blocks = table.shape[0]
    return pl.pallas_call(
        lambda *refs: serve_kernel(slots, *refs),
        out_shape=jax.ShapeDtypeStruct((2 * rows, columns), jnp.float32),
        in_specs=[IN_VMEM] * 3,
        out_specs=IN_VMEM,
        compiler_params=pltpu.CompilerParams(vmem_limit_bytes=16 * MIB),
        cost_estimate=pl.CostEstimate(
            flops=4 * rows * blocks * columns,
            bytes_accessed=16 * rows * columns,
            transcendentals=0,
        ),
        name="serve",
    )(wanted, table, own)


def add_up_kernel(kinds, index_ref, rows_ref, orbit_ref, out_ref):
    groups, lanes = index_ref.shape
    blocks = out_ref.shape[0]
    peers = rows_ref.shape[0] // kinds
    rows = jnp.concatenate([two_parts(rows_ref[pl.ds(k, peers, stride=kinds), :]) for k in range(kinds)], axis=0)
    step = 128
    block = lax.broadcasted_iota(jnp.int32, (step, lanes), 0)
    for start in range(0, blocks, step):
        marks = jnp.concatenate([ones_where(block + start == index_ref[g : g + 1, :]) for g in range(groups)], axis=1)
        product = jnp.dot(marks, rows, preferred_element_type=jnp.float32)
        part = slice(start, start + step)
        out_ref[part, :] = halves_added(product) / orbit_factor(orbit_ref[part, :])


def add_up(index, rows, orbit, kinds):
    blocks, columns = orbit.shape
    count = rows.shape[0]
    return pl.pallas_call(
        lambda *refs: add_up_kernel(kinds, *refs),
        out_shape=jax.ShapeDtypeStruct((blocks, columns), jnp.float32),
        in_specs=[IN_VMEM] * 3,
        out_specs=IN_VMEM,
        compiler_params=pltpu.CompilerParams(vmem_limit_bytes=16 * MIB),
        cost_estimate=pl.CostEstimate(
            flops=4 * count * blocks * columns,
            bytes_accessed=(count + 2 * blocks) * columns * 4,
            transcendentals=blocks * columns,
        ),
        name="add_up",
    )(index, rows, orbit)


def per_device(amplitudes, orbit_index, requests, targets):
    columns = amplitudes.shape[1]
    nx, ny, nz, nc = (lax.axis_size(a) for a in AXES)
    plane = nx * ny * nc
    slots = requests.shape[-1]
    asked = requests.reshape(nx, ny, nz, nc, slots).transpose(0, 1, 3, 4, 2)
    asked = asked.reshape(plane, slots, nz)
    asked = lax.all_to_all(asked, PLANE, split_axis=0, concat_axis=0, tiled=True)
    asked = asked.transpose(2, 1, 0)
    wanted = lax.all_to_all(asked, "z", split_axis=0, concat_axis=0, tiled=True)
    places = targets.reshape(nx, ny, nz, nc, slots).transpose(2, 4, 0, 1, 3)
    places = places.reshape(nz, slots, plane)
    table, own = own_rows(
        amplitudes, orbit_index, places.reshape(nz * slots, plane), slots
    )
    outgoing = serve(wanted.reshape(nz * slots, plane), table, own, slots)
    arrived = lax.all_to_all(
        outgoing.reshape(nz * plane, 2 * slots, columns),
        PEERS,
        split_axis=0,
        concat_axis=0,
        tiled=True,
    )
    landing = jnp.concatenate([wanted, places], axis=1).transpose(1, 0, 2)
    return add_up(
        landing.reshape(-1, 128), arrived.reshape(-1, columns), orbit_index, 2 * slots
    )


def solution(mesh):
    groups, shards = mesh.devices.shape
    devices = mesh.devices.reshape(groups, 4, shards // 8, 2)
    split = P(AXES)
    return jax.shard_map(
        per_device,
        mesh=Mesh(devices, AXES),
        in_specs=(split, split, split, split),
        out_specs=split,
        check_vma=False,
    )
```

```python
import jax
import jax.numpy as jnp
from jax import lax
from jax.experimental import pallas as pl
from jax.experimental.pallas import tpu as pltpu
from jax.sharding import Mesh
from jax.sharding import PartitionSpec as P

AXES = ("x", "y", "z", "c")
PEERS = ("z", "c", "x", "y")
PLANE = ("c", "x", "y")
IN_VMEM = pl.BlockSpec(memory_space=pltpu.VMEM)
MIB = 2**20
STEP = 8


def orbit_factor(orbit):
    return jnp.sqrt(96.0 * jnp.exp2(-orbit.astype(jnp.float32)))


def two_parts(values):
    high = values.astype(jnp.bfloat16)
    low = (values - high.astype(jnp.float32)).astype(jnp.bfloat16)
    return jnp.concatenate([high, low], axis=1)


def halves_added(product):
    columns = product.shape[1] // 2
    return product[:, :columns] + product[:, columns:]


def ones_where(hit):
    return jnp.where(hit, 1.0, 0.0).astype(jnp.bfloat16)


def lanes_joined(pieces, lanes):
    share = lanes // pieces[0].shape[1]
    rows = [
        jnp.concatenate(pieces[start : start + share], axis=1)
        for start in range(0, len(pieces), share)
    ]
    return jnp.concatenate(rows, axis=0)


def every_other(values, first):
    lanes = values.shape[1]
    lane = lax.broadcasted_iota(jnp.int32, values.shape, 1)
    if first:
        values = pltpu.roll(values, lanes - 1, 1)
    for bit in range(4):
        moved = pltpu.roll(values, lanes - (1 << bit), 1)
        values = jnp.where((lane >> bit) & 1 == 1, moved, values)
    return values


def deal_kernel(asked_ref, out_ref):
    slots, total = asked_ref.shape
    peers, _, lines = out_ref.shape
    columns = peers // 2
    run = total // columns
    for start in range(0, total, 128):
        whole = asked_ref[:, start : start + 128]
        for core in range(2):
            sorted_out = every_other(whole, core)
            for part in range(0, 128, run):
                column = (start + part) // run
                out_ref[core * columns + column] = sorted_out[:, part : part + lines]


def deal(asked, peers, lines):
    slots = asked.shape[0]
    return pl.pallas_call(
        deal_kernel,
        out_shape=jax.ShapeDtypeStruct((peers, slots, lines), jnp.int32),
        in_specs=[IN_VMEM],
        out_specs=IN_VMEM,
        compiler_params=pltpu.CompilerParams(vmem_limit_bytes=4 * MIB),
        cost_estimate=pl.CostEstimate(flops=40960, bytes_accessed=40960, transcendentals=0),
        name="deal",
    )(asked)


def picked(columns, table, step):
    width = columns[0].shape[0]
    blocks = table.shape[0]
    block = lax.broadcasted_iota(jnp.int32, (width, blocks), 1)
    for first in range(0, len(columns), step):
        chosen = [ones_where(column == block) for column in columns[first : first + step]]
        product = jnp.dot(
            jnp.concatenate(chosen, axis=0), table, preferred_element_type=jnp.float32
        )
        yield first * width, halves_added(product)


def own_kernel(amplitudes_ref, orbit_ref, places_ref, table_ref, own_ref, landing_ref):
    table_ref[...] = two_parts(amplitudes_ref[...] * orbit_factor(orbit_ref[...]))
    slots, total = places_ref.shape
    run = 32
    lanes = landing_ref.shape[1]
    columns = []
    for slot in range(slots):
        grid = jnp.concatenate(
            [places_ref[slot : slot + 1, start : start + run] for start in range(0, total, run)],
            axis=0,
        )
        columns += [grid[:, column : column + 1] for column in range(run)]
        turned = grid.T
        share = total // lanes
        landing_ref[slot * share : (slot + 1) * share, :] = lanes_joined(
            [turned[row : row + 1, :] for row in range(run)], lanes
        )
    for first, rows in picked(columns, table_ref[...], 16):
        own_ref[first : first + rows.shape[0], :] = rows


def own_rows(amplitudes, orbit, places):
    blocks, columns = amplitudes.shape
    rows = places.size
    return pl.pallas_call(
        own_kernel,
        out_shape=(
            jax.ShapeDtypeStruct((blocks, 2 * columns), jnp.bfloat16),
            jax.ShapeDtypeStruct((rows, columns), jnp.float32),
            jax.ShapeDtypeStruct((rows // 128, 128), jnp.int32),
        ),
        in_specs=[IN_VMEM] * 3,
        out_specs=(IN_VMEM,) * 3,
        compiler_params=pltpu.CompilerParams(vmem_limit_bytes=16 * MIB),
        cost_estimate=pl.CostEstimate(
            flops=4 * rows * blocks * columns,
            bytes_accessed=20 * blocks * columns,
            transcendentals=blocks * columns,
        ),
        name="own_rows",
    )(amplitudes, orbit, places)


def serve_kernel(wanted_ref, table_ref, own_ref, out_ref, landing_ref):
    lines, slots, width = wanted_ref.shape
    lanes = landing_ref.shape[1]
    peers = lines * width
    share = peers // lanes
    for slot in range(slots):
        part = slice(slot * peers, (slot + 1) * peers)
        out_ref[pl.ds(slot, peers, stride=2 * slots), :] = own_ref[part, :]
    numbers = [wanted_ref[:, slot, :] for slot in range(slots)]
    turned = [number.T for number in numbers]
    columns = [turn[:, line : line + 1] for turn in turned for line in range(lines)]
    for first, rows in picked(columns, table_ref[...], 8):
        slot, start = divmod(first, peers)
        out_ref[
            pl.ds(start * 2 * slots + slots + slot, rows.shape[0], stride=2 * slots), :
        ] = rows
    for slot in range(slots):
        landing_ref[slot * share : (slot + 1) * share, :] = lanes_joined(
            [numbers[slot][line : line + 1, :] for line in range(lines)], lanes
        )


def serve(wanted, table, own):
    rows, columns = own.shape
    blocks = table.shape[0]
    return pl.pallas_call(
        serve_kernel,
        out_shape=(
            jax.ShapeDtypeStruct((2 * rows, columns), jnp.float32),
            jax.ShapeDtypeStruct((rows // 128, 128), jnp.int32),
        ),
        in_specs=[IN_VMEM] * 3,
        out_specs=(IN_VMEM,) * 2,
        compiler_params=pltpu.CompilerParams(vmem_limit_bytes=16 * MIB),
        cost_estimate=pl.CostEstimate(
            flops=4 * rows * blocks * columns,
            bytes_accessed=16 * rows * columns,
            transcendentals=0,
        ),
        name="serve",
    )(wanted, table, own)


def add_up_kernel(first_ref, second_ref, rows_ref, orbit_ref, out_ref):
    groups, lanes = first_ref.shape
    blocks = out_ref.shape[0]
    count = rows_ref.shape[0]
    peers = groups * lanes // 2
    kinds = count // peers
    rows = jnp.concatenate(
        [two_parts(rows_ref[pl.ds(kind, peers, stride=kinds), :]) for kind in range(kinds)],
        axis=0,
    )
    index = [ref[group : group + 1, :] for ref in (first_ref, second_ref) for group in range(groups)]
    step = 128
    block = lax.broadcasted_iota(jnp.int32, (step, lanes), 0)
    for start in range(0, blocks, step):
        marks = jnp.concatenate(
            [ones_where(block + start == numbers) for numbers in index], axis=1
        )
        product = jnp.dot(marks, rows, preferred_element_type=jnp.float32)
        part = slice(start, start + step)
        out_ref[part, :] = halves_added(product) / orbit_factor(orbit_ref[part, :])


def add_up(first, second, rows, orbit):
    blocks, columns = orbit.shape
    count = rows.shape[0]
    return pl.pallas_call(
        add_up_kernel,
        out_shape=jax.ShapeDtypeStruct((blocks, columns), jnp.float32),
        in_specs=[IN_VMEM] * 4,
        out_specs=IN_VMEM,
        compiler_params=pltpu.CompilerParams(vmem_limit_bytes=16 * MIB),
        cost_estimate=pl.CostEstimate(
            flops=4 * count * blocks * columns,
            bytes_accessed=(count + 2 * blocks) * columns * 4,
            transcendentals=blocks * columns,
        ),
        name="add_up",
    )(first, second, rows, orbit)


def per_device(amplitudes, orbit_index, requests, targets):
    columns = amplitudes.shape[1]
    nx, ny, nz, nc = (lax.axis_size(a) for a in AXES)
    plane = nx * ny * nc
    slots = requests.shape[-1]
    asked = deal(requests.reshape(-1, slots).T, plane, nz)
    asked = lax.all_to_all(asked, PLANE, split_axis=0, concat_axis=0, tiled=True)
    wanted = lax.all_to_all(
        asked.transpose(2, 1, 0), "z", split_axis=0, concat_axis=0, tiled=True
    )
    table, own, landing = own_rows(amplitudes, orbit_index, targets.reshape(-1, slots).T)
    outgoing, wanted_landing = serve(wanted, table, own)
    arrived = lax.all_to_all(
        outgoing.reshape(nz * plane, 2 * slots, columns),
        PEERS,
        split_axis=0,
        concat_axis=0,
        tiled=True,
    )
    return add_up(wanted_landing, landing, arrived.reshape(-1, columns), orbit_index)


def solution(mesh):
    groups, shards = mesh.devices.shape
    devices = mesh.devices.reshape(groups, 4, shards // 8, 2)
    split = P(AXES)
    return jax.shard_map(
        per_device,
        mesh=Mesh(devices, AXES),
        in_specs=(split, split, split, split),
        out_specs=split,
        check_vma=False,
    )
```

```python
import jax
import jax.numpy as jnp
from jax import lax
from jax.experimental import pallas as pl
from jax.experimental.pallas import tpu as pltpu
from jax.sharding import Mesh
from jax.sharding import PartitionSpec as P

AXES = ("x", "y", "z", "c")
PEERS = ("z", "c", "x", "y")
PLANE = ("c", "x", "y")
IN_VMEM = pl.BlockSpec(memory_space=pltpu.VMEM)
MIB = 2**20
STEP = 8


def orbit_factor(orbit):
    return jnp.sqrt(96.0 * jnp.exp2(-orbit.astype(jnp.float32)))


def two_parts(values):
    high = values.astype(jnp.bfloat16)
    low = (values - high.astype(jnp.float32)).astype(jnp.bfloat16)
    return jnp.concatenate([high, low], axis=1)


def halves_added(product):
    columns = product.shape[1] // 2
    return product[:, :columns] + product[:, columns:]


def ones_where(hit):
    return jnp.where(hit, jnp.bfloat16(1.0), jnp.bfloat16(0.0))


def lanes_joined(pieces, lanes):
    share = lanes // pieces[0].shape[1]
    rows = [
        jnp.concatenate(pieces[start : start + share], axis=1)
        for start in range(0, len(pieces), share)
    ]
    return jnp.concatenate(rows, axis=0)


def every_other(values, first):
    lanes = values.shape[1]
    lane = lax.broadcasted_iota(jnp.int32, values.shape, 1)
    if first:
        values = pltpu.roll(values, lanes - 1, 1)
    for bit in range(4):
        moved = pltpu.roll(values, lanes - (1 << bit), 1)
        values = jnp.where((lane >> bit) & 1 == 1, moved, values)
    return values


def deal_kernel(asked_ref, out_ref):
    slots, total = asked_ref.shape
    peers, _, lines = out_ref.shape
    columns = peers // 2
    run = total // columns
    for start in range(0, total, 128):
        whole = asked_ref[:, start : start + 128]
        for core in range(2):
            sorted_out = every_other(whole, core)
            for part in range(0, 128, run):
                column = (start + part) // run
                out_ref[core * columns + column] = sorted_out[:, part : part + lines]


def deal(asked, peers, lines):
    slots = asked.shape[0]
    return pl.pallas_call(
        deal_kernel,
        out_shape=jax.ShapeDtypeStruct((peers, slots, lines), jnp.int32),
        in_specs=[IN_VMEM],
        out_specs=IN_VMEM,
        compiler_params=pltpu.CompilerParams(vmem_limit_bytes=4 * MIB),
        cost_estimate=pl.CostEstimate(flops=40960, bytes_accessed=40960, transcendentals=0),
        name="deal",
    )(asked)


def picked(columns, table, step):
    width = columns[0].shape[0]
    blocks = table.shape[0]
    block = lax.broadcasted_iota(jnp.int32, (width, blocks), 1).astype(jnp.int16)
    for first in range(0, len(columns), step):
        chosen = [ones_where(column.astype(jnp.int16) == block) for column in columns[first : first + step]]
        product = jnp.dot(
            jnp.concatenate(chosen, axis=0), table, preferred_element_type=jnp.float32
        )
        yield first * width, halves_added(product)


def own_kernel(weighted_ref, places_ref, table_ref, own_ref, landing_ref):
    table_ref[...] = two_parts(weighted_ref[...])
    slots, total = places_ref.shape
    run = 32
    lanes = landing_ref.shape[1]
    columns = []
    for slot in range(slots):
        grid = jnp.concatenate(
            [places_ref[slot : slot + 1, start : start + run] for start in range(0, total, run)],
            axis=0,
        )
        columns += [grid[:, column : column + 1] for column in range(run)]
        turned = grid.T
        share = total // lanes
        landing_ref[slot * share : (slot + 1) * share, :] = lanes_joined(
            [turned[row : row + 1, :] for row in range(run)], lanes
        )
    for first, rows in picked(columns, table_ref[...], 16):
        own_ref[first : first + rows.shape[0], :] = rows


def own_rows(weighted, places):
    blocks, columns = weighted.shape
    rows = places.size
    return pl.pallas_call(
        own_kernel,
        out_shape=(
            jax.ShapeDtypeStruct((blocks, 2 * columns), jnp.bfloat16),
            jax.ShapeDtypeStruct((rows, columns), jnp.float32),
            jax.ShapeDtypeStruct((rows // 128, 128), jnp.int32),
        ),
        in_specs=[IN_VMEM] * 2,
        out_specs=(IN_VMEM,) * 3,
        compiler_params=pltpu.CompilerParams(vmem_limit_bytes=16 * MIB),
        cost_estimate=pl.CostEstimate(
            flops=4 * rows * blocks * columns,
            bytes_accessed=16 * blocks * columns,
            transcendentals=0,
        ),
        name="own_rows",
    )(weighted, places)


def serve_kernel(wanted_ref, table_ref, own_ref, out_ref, landing_ref):
    lines, slots, width = wanted_ref.shape
    lanes = landing_ref.shape[1]
    peers = lines * width
    share = peers // lanes
    for slot in range(slots):
        part = slice(slot * peers, (slot + 1) * peers)
        out_ref[pl.ds(slot, peers, stride=2 * slots), :] = own_ref[part, :]
    numbers = [wanted_ref[:, slot, :] for slot in range(slots)]
    turned = [number.T for number in numbers]
    columns = [turn[:, line : line + 1] for turn in turned for line in range(lines)]
    for first, rows in picked(columns, table_ref[...], 8):
        slot, start = divmod(first, peers)
        out_ref[
            pl.ds(start * 2 * slots + slots + slot, rows.shape[0], stride=2 * slots), :
        ] = rows
    for slot in range(slots):
        landing_ref[slot * share : (slot + 1) * share, :] = lanes_joined(
            [numbers[slot][line : line + 1, :] for line in range(lines)], lanes
        )


def serve(wanted, table, own):
    rows, columns = own.shape
    blocks = table.shape[0]
    return pl.pallas_call(
        serve_kernel,
        out_shape=(
            jax.ShapeDtypeStruct((2 * rows, columns), jnp.float32),
            jax.ShapeDtypeStruct((rows // 128, 128), jnp.int32),
        ),
        in_specs=[IN_VMEM] * 3,
        out_specs=(IN_VMEM,) * 2,
        compiler_params=pltpu.CompilerParams(vmem_limit_bytes=16 * MIB),
        cost_estimate=pl.CostEstimate(
            flops=4 * rows * blocks * columns,
            bytes_accessed=16 * rows * columns,
            transcendentals=0,
        ),
        name="serve",
    )(wanted, table, own)


def add_up_kernel(first_ref, second_ref, rows_ref, orbit_ref, out_ref):
    groups, lanes = first_ref.shape
    blocks = out_ref.shape[0]
    count = rows_ref.shape[0]
    peers = groups * lanes // 2
    kinds = count // peers
    rows = jnp.concatenate(
        [two_parts(rows_ref[pl.ds(kind, peers, stride=kinds), :]) for kind in range(kinds)],
        axis=0,
    )
    index = [ref[group : group + 1, :] for ref in (first_ref, second_ref) for group in range(groups)]
    step = 256
    block = lax.broadcasted_iota(jnp.int32, (step, lanes), 0)
    index = [jnp.broadcast_to(numbers, (step, lanes)).astype(jnp.int16) for numbers in index]
    for start in range(0, blocks, step):
        marks = jnp.concatenate(
            [ones_where((block + start).astype(jnp.int16) == numbers) for numbers in index], axis=1
        )
        product = jnp.dot(marks, rows, preferred_element_type=jnp.float32)
        part = slice(start, start + step)
        out_ref[part, :] = halves_added(product) / orbit_factor(orbit_ref[part, :])


def add_up(first, second, rows, orbit):
    blocks, columns = orbit.shape
    count = rows.shape[0]
    return pl.pallas_call(
        add_up_kernel,
        out_shape=jax.ShapeDtypeStruct((blocks, columns), jnp.float32),
        in_specs=[IN_VMEM] * 4,
        out_specs=IN_VMEM,
        compiler_params=pltpu.CompilerParams(vmem_limit_bytes=16 * MIB),
        cost_estimate=pl.CostEstimate(
            flops=4 * count * blocks * columns,
            bytes_accessed=(count + 2 * blocks) * columns * 4,
            transcendentals=blocks * columns,
        ),
        name="add_up",
    )(first, second, rows, orbit)


def per_device(amplitudes, orbit_index, requests, targets):
    columns = amplitudes.shape[1]
    nx, ny, nz, nc = (lax.axis_size(a) for a in AXES)
    plane = nx * ny * nc
    slots = requests.shape[-1]
    asked = deal(requests.reshape(-1, slots).T, plane, nz)
    asked = lax.all_to_all(asked, PLANE, split_axis=0, concat_axis=0, tiled=True)
    wanted = lax.all_to_all(
        asked.transpose(2, 1, 0), "z", split_axis=0, concat_axis=0, tiled=True
    )
    weighted = amplitudes * orbit_factor(orbit_index)
    table, own, landing = own_rows(weighted, targets.reshape(-1, slots).T)
    outgoing, wanted_landing = serve(wanted, table, own)
    arrived = lax.all_to_all(
        outgoing.reshape(nz * plane, 2 * slots, columns),
        PEERS,
        split_axis=0,
        concat_axis=0,
        tiled=True,
    )
    return add_up(wanted_landing, landing, arrived.reshape(-1, columns), orbit_index)


def solution(mesh):
    groups, shards = mesh.devices.shape
    devices = mesh.devices.reshape(groups, 4, shards // 8, 2)
    split = P(AXES)
    return jax.shard_map(
        per_device,
        mesh=Mesh(devices, AXES),
        in_specs=(split, split, split, split),
        out_specs=split,
        check_vma=False,
    )
```

```python
import jax
import jax.numpy as jnp
from jax import lax
from jax.experimental import pallas as pl
from jax.experimental.pallas import tpu as pltpu
from jax.sharding import Mesh
from jax.sharding import PartitionSpec as P

AXES = ("x", "y", "z", "c")
PEERS = ("z", "c", "x", "y")
PLANE = ("c", "x", "y")
IN_VMEM = pl.BlockSpec(memory_space=pltpu.VMEM)
MIB = 2**20
STEP = 8


def orbit_factor(orbit):
    return jnp.sqrt(96.0 * jnp.exp2(-orbit.astype(jnp.float32)))


def two_parts(values):
    high = values.astype(jnp.bfloat16)
    low = (values - high.astype(jnp.float32)).astype(jnp.bfloat16)
    return jnp.concatenate([high, low], axis=1)


def halves_added(product):
    columns = product.shape[1] // 2
    return product[:, :columns] + product[:, columns:]


def ones_where(hit):
    return jnp.where(hit, jnp.bfloat16(1.0), jnp.bfloat16(0.0))


def lanes_joined(pieces, lanes):
    share = lanes // pieces[0].shape[1]
    rows = [
        jnp.concatenate(pieces[start : start + share], axis=1)
        for start in range(0, len(pieces), share)
    ]
    return jnp.concatenate(rows, axis=0)


def every_other(values, first):
    lanes = values.shape[1]
    lane = lax.broadcasted_iota(jnp.int32, values.shape, 1)
    if first:
        values = pltpu.roll(values, lanes - 1, 1)
    for bit in range(4):
        moved = pltpu.roll(values, lanes - (1 << bit), 1)
        values = jnp.where((lane >> bit) & 1 == 1, moved, values)
    return values


def deal_kernel(asked_ref, out_ref):
    slots, total = asked_ref.shape
    peers, _, lines = out_ref.shape
    columns = peers // 2
    run = total // columns
    for start in range(0, total, 128):
        whole = asked_ref[:, start : start + 128]
        for core in range(2):
            sorted_out = every_other(whole, core)
            for part in range(0, 128, run):
                column = (start + part) // run
                out_ref[core * columns + column] = sorted_out[:, part : part + lines]


def deal(asked, peers, lines):
    slots = asked.shape[0]
    return pl.pallas_call(
        deal_kernel,
        out_shape=jax.ShapeDtypeStruct((peers, slots, lines), jnp.int32),
        in_specs=[IN_VMEM],
        out_specs=IN_VMEM,
        compiler_params=pltpu.CompilerParams(vmem_limit_bytes=4 * MIB),
        cost_estimate=pl.CostEstimate(flops=40960, bytes_accessed=40960, transcendentals=0),
        name="deal",
    )(asked)


def picked(columns, table, step):
    width = columns[0].shape[0]
    blocks = table.shape[0]
    block = lax.broadcasted_iota(jnp.int32, (width, blocks), 1).astype(jnp.int16)
    for first in range(0, len(columns), step):
        chosen = [ones_where(column.astype(jnp.int16) == block) for column in columns[first : first + step]]
        product = jnp.dot(
            jnp.concatenate(chosen, axis=0), table, preferred_element_type=jnp.float32
        )
        yield first * width, halves_added(product)


def own_kernel(amplitudes_ref, orbit_ref, places_ref, table_ref, own_ref, landing_ref):
    table_ref[...] = two_parts(amplitudes_ref[...] * orbit_factor(orbit_ref[...]))
    slots, total = places_ref.shape
    run = 32
    lanes = landing_ref.shape[1]
    columns = []
    for slot in range(slots):
        grid = jnp.concatenate(
            [places_ref[slot : slot + 1, start : start + run] for start in range(0, total, run)],
            axis=0,
        )
        columns += [grid[:, column : column + 1] for column in range(run)]
        turned = grid.T
        share = total // lanes
        landing_ref[slot * share : (slot + 1) * share, :] = lanes_joined(
            [turned[row : row + 1, :] for row in range(run)], lanes
        )
    for first, rows in picked(columns, table_ref[...], 16):
        own_ref[first : first + rows.shape[0], :] = rows


def own_rows(amplitudes, orbit, places):
    blocks, columns = amplitudes.shape
    rows = places.size
    return pl.pallas_call(
        own_kernel,
        out_shape=(
            jax.ShapeDtypeStruct((blocks, 2 * columns), jnp.bfloat16),
            jax.ShapeDtypeStruct((rows, columns), jnp.float32),
            jax.ShapeDtypeStruct((rows // 128, 128), jnp.int32),
        ),
        in_specs=[IN_VMEM] * 3,
        out_specs=(IN_VMEM,) * 3,
        compiler_params=pltpu.CompilerParams(vmem_limit_bytes=16 * MIB),
        cost_estimate=pl.CostEstimate(
            flops=4 * rows * blocks * columns,
            bytes_accessed=20 * blocks * columns,
            transcendentals=blocks * columns,
        ),
        name="own_rows",
    )(amplitudes, orbit, places)


def serve_kernel(wanted_ref, table_ref, own_ref, out_ref, landing_ref):
    lines, slots, width = wanted_ref.shape
    lanes = landing_ref.shape[1]
    peers = lines * width
    share = peers // lanes
    for slot in range(slots):
        part = slice(slot * peers, (slot + 1) * peers)
        out_ref[pl.ds(slot, peers, stride=2 * slots), :] = own_ref[part, :]
    numbers = [wanted_ref[:, slot, :] for slot in range(slots)]
    turned = [number.T for number in numbers]
    columns = [turn[:, line : line + 1] for turn in turned for line in range(lines)]
    for first, rows in picked(columns, table_ref[...], 8):
        slot, start = divmod(first, peers)
        out_ref[
            pl.ds(start * 2 * slots + slots + slot, rows.shape[0], stride=2 * slots), :
        ] = rows
    for slot in range(slots):
        landing_ref[slot * share : (slot + 1) * share, :] = lanes_joined(
            [numbers[slot][line : line + 1, :] for line in range(lines)], lanes
        )


def serve(wanted, table, own):
    rows, columns = own.shape
    blocks = table.shape[0]
    return pl.pallas_call(
        serve_kernel,
        out_shape=(
            jax.ShapeDtypeStruct((2 * rows, columns), jnp.float32),
            jax.ShapeDtypeStruct((rows // 128, 128), jnp.int32),
        ),
        in_specs=[IN_VMEM] * 3,
        out_specs=(IN_VMEM,) * 2,
        compiler_params=pltpu.CompilerParams(vmem_limit_bytes=16 * MIB),
        cost_estimate=pl.CostEstimate(
            flops=4 * rows * blocks * columns,
            bytes_accessed=16 * rows * columns,
            transcendentals=0,
        ),
        name="serve",
    )(wanted, table, own)


def add_up_kernel(first_ref, second_ref, rows_ref, orbit_ref, out_ref):
    groups, lanes = first_ref.shape
    blocks = out_ref.shape[0]
    count = rows_ref.shape[0]
    peers = groups * lanes // 2
    kinds = count // peers
    rows = jnp.concatenate(
        [two_parts(rows_ref[pl.ds(kind, peers, stride=kinds), :]) for kind in range(kinds)],
        axis=0,
    )
    index = [ref[group : group + 1, :] for ref in (first_ref, second_ref) for group in range(groups)]
    step = 256
    block = lax.broadcasted_iota(jnp.int32, (step, lanes), 0)
    index = [jnp.broadcast_to(numbers, (step, lanes)).astype(jnp.int16) for numbers in index]
    for start in range(0, blocks, step):
        marks = jnp.concatenate(
            [ones_where((block + start).astype(jnp.int16) == numbers) for numbers in index], axis=1
        )
        product = jnp.dot(marks, rows, preferred_element_type=jnp.float32)
        part = slice(start, start + step)
        out_ref[part, :] = halves_added(product) / orbit_factor(orbit_ref[part, :])


def add_up(first, second, rows, orbit):
    blocks, columns = orbit.shape
    count = rows.shape[0]
    return pl.pallas_call(
        add_up_kernel,
        out_shape=jax.ShapeDtypeStruct((blocks, columns), jnp.float32),
        in_specs=[IN_VMEM] * 4,
        out_specs=IN_VMEM,
        compiler_params=pltpu.CompilerParams(vmem_limit_bytes=16 * MIB),
        cost_estimate=pl.CostEstimate(
            flops=4 * count * blocks * columns,
            bytes_accessed=(count + 2 * blocks) * columns * 4,
            transcendentals=blocks * columns,
        ),
        name="add_up",
    )(first, second, rows, orbit)


def per_device(amplitudes, orbit_index, requests, targets):
    columns = amplitudes.shape[1]
    nx, ny, nz, nc = (lax.axis_size(a) for a in AXES)
    plane = nx * ny * nc
    slots = requests.shape[-1]
    asked = deal(requests.reshape(-1, slots).T, plane, nz)
    asked = lax.all_to_all(asked, PLANE, split_axis=0, concat_axis=0, tiled=True)
    wanted = lax.all_to_all(
        asked.transpose(2, 1, 0), "z", split_axis=0, concat_axis=0, tiled=True
    )
    table, own, landing = own_rows(amplitudes, orbit_index, targets.reshape(-1, slots).T)
    outgoing, wanted_landing = serve(wanted, table, own)
    arrived = lax.all_to_all(
        outgoing.reshape(nz * plane, 2 * slots, columns),
        PEERS,
        split_axis=0,
        concat_axis=0,
        tiled=True,
    )
    return add_up(wanted_landing, landing, arrived.reshape(-1, columns), orbit_index)


def solution(mesh):
    groups, shards = mesh.devices.shape
    devices = mesh.devices.reshape(groups, 4, shards // 8, 2)
    split = P(AXES)
    return jax.shard_map(
        per_device,
        mesh=Mesh(devices, AXES),
        in_specs=(split, split, split, split),
        out_specs=split,
        check_vma=False,
    )
```

```python
import jax
import jax.numpy as jnp
from jax import lax
from jax.experimental import pallas as pl
from jax.experimental.pallas import tpu as pltpu
from jax.sharding import Mesh
from jax.sharding import PartitionSpec as P

AXES = ("x", "y", "z", "c")
PEERS = ("z", "c", "x", "y")
PLANE = ("c", "x", "y")
IN_VMEM = pl.BlockSpec(memory_space=pltpu.VMEM)
MIB = 2**20
STEP = 8


def orbit_factor(orbit):
    return jnp.sqrt(96.0 * jnp.exp2(-orbit.astype(jnp.float32)))


def two_parts(values):
    high = values.astype(jnp.bfloat16)
    low = (values - high.astype(jnp.float32)).astype(jnp.bfloat16)
    return jnp.concatenate([high, low], axis=1)


def halves_added(product):
    columns = product.shape[1] // 2
    return product[:, :columns] + product[:, columns:]


def ones_where(hit):
    return jnp.where(hit, jnp.bfloat16(1.0), jnp.bfloat16(0.0))


def lanes_joined(pieces, lanes):
    share = lanes // pieces[0].shape[1]
    rows = [
        jnp.concatenate(pieces[start : start + share], axis=1)
        for start in range(0, len(pieces), share)
    ]
    return jnp.concatenate(rows, axis=0)


def deal_kernel(asked_ref, out_ref):
    slots, total = asked_ref.shape
    lines, _, width = out_ref.shape
    run = 32
    for slot in range(slots):
        grid = jnp.concatenate(
            [asked_ref[slot : slot + 1, start : start + run] for start in range(0, total, run)],
            axis=0,
        )
        turned = grid.T
        cores = run // lines
        for line in range(lines):
            out_ref[line, slot : slot + 1, :] = jnp.concatenate(
                [turned[line * cores + core : line * cores + core + 1, :] for core in range(cores)],
                axis=1,
            )


def deal(asked, lines):
    slots, total = asked.shape
    return pl.pallas_call(
        deal_kernel,
        out_shape=jax.ShapeDtypeStruct((lines, slots, total // lines), jnp.int32),
        in_specs=[IN_VMEM],
        out_specs=IN_VMEM,
        compiler_params=pltpu.CompilerParams(vmem_limit_bytes=4 * MIB),
        cost_estimate=pl.CostEstimate(flops=40960, bytes_accessed=40960, transcendentals=0),
        name="deal",
    )(asked)


def picked(columns, table, step):
    width = columns[0].shape[0]
    blocks = table.shape[0]
    block = lax.broadcasted_iota(jnp.int32, (width, blocks), 1).astype(jnp.int16)
    for first in range(0, len(columns), step):
        chosen = [ones_where(column.astype(jnp.int16) == block) for column in columns[first : first + step]]
        product = jnp.dot(
            jnp.concatenate(chosen, axis=0), table, preferred_element_type=jnp.float32
        )
        yield first * width, halves_added(product)


def own_kernel(amplitudes_ref, orbit_ref, places_ref, table_ref, own_ref, landing_ref):
    table_ref[...] = two_parts(amplitudes_ref[...] * orbit_factor(orbit_ref[...]))
    slots, total = places_ref.shape
    run = 32
    lanes = landing_ref.shape[1]
    columns = []
    for slot in range(slots):
        grid = jnp.concatenate(
            [places_ref[slot : slot + 1, start : start + run] for start in range(0, total, run)],
            axis=0,
        )
        columns += [grid[:, column : column + 1] for column in range(run)]
        turned = grid.T
        share = total // lanes
        landing_ref[slot * share : (slot + 1) * share, :] = lanes_joined(
            [turned[row : row + 1, :] for row in range(run)], lanes
        )
    for first, rows in picked(columns, table_ref[...], 16):
        own_ref[first : first + rows.shape[0], :] = rows


def own_rows(amplitudes, orbit, places):
    blocks, columns = amplitudes.shape
    rows = places.size
    return pl.pallas_call(
        own_kernel,
        out_shape=(
            jax.ShapeDtypeStruct((blocks, 2 * columns), jnp.bfloat16),
            jax.ShapeDtypeStruct((rows, columns), jnp.float32),
            jax.ShapeDtypeStruct((rows // 128, 128), jnp.int32),
        ),
        in_specs=[IN_VMEM] * 3,
        out_specs=(IN_VMEM,) * 3,
        compiler_params=pltpu.CompilerParams(vmem_limit_bytes=16 * MIB),
        cost_estimate=pl.CostEstimate(
            flops=4 * rows * blocks * columns,
            bytes_accessed=20 * blocks * columns,
            transcendentals=blocks * columns,
        ),
        name="own_rows",
    )(amplitudes, orbit, places)


def serve_kernel(wanted_ref, table_ref, own_ref, out_ref, landing_ref):
    width, slots, lines = wanted_ref.shape
    lanes = landing_ref.shape[1]
    peers = lines * width
    share = peers // lanes
    for slot in range(slots):
        part = slice(slot * peers, (slot + 1) * peers)
        out_ref[pl.ds(slot, peers, stride=2 * slots), :] = own_ref[part, :]
    whole = jnp.concatenate([wanted_ref[:, slot, :] for slot in range(slots)], axis=1)
    square = whole.T
    numbers = [square[slot * lines : (slot + 1) * lines, :] for slot in range(slots)]
    turned = [whole[:, slot * lines : (slot + 1) * lines] for slot in range(slots)]
    columns = [turn[:, line : line + 1] for turn in turned for line in range(lines)]
    for first, rows in picked(columns, table_ref[...], 8):
        slot, start = divmod(first, peers)
        out_ref[
            pl.ds(start * 2 * slots + slots + slot, rows.shape[0], stride=2 * slots), :
        ] = rows
    for slot in range(slots):
        landing_ref[slot * share : (slot + 1) * share, :] = lanes_joined(
            [numbers[slot][line : line + 1, :] for line in range(lines)], lanes
        )


def serve(wanted, table, own):
    rows, columns = own.shape
    blocks = table.shape[0]
    return pl.pallas_call(
        serve_kernel,
        out_shape=(
            jax.ShapeDtypeStruct((2 * rows, columns), jnp.float32),
            jax.ShapeDtypeStruct((rows // 128, 128), jnp.int32),
        ),
        in_specs=[IN_VMEM] * 3,
        out_specs=(IN_VMEM,) * 2,
        compiler_params=pltpu.CompilerParams(vmem_limit_bytes=16 * MIB),
        cost_estimate=pl.CostEstimate(
            flops=4 * rows * blocks * columns,
            bytes_accessed=16 * rows * columns,
            transcendentals=0,
        ),
        name="serve",
    )(wanted, table, own)


def add_up_kernel(first_ref, second_ref, rows_ref, orbit_ref, out_ref):
    groups, lanes = first_ref.shape
    blocks = out_ref.shape[0]
    count = rows_ref.shape[0]
    peers = groups * lanes // 2
    kinds = count // peers
    rows = jnp.concatenate(
        [two_parts(rows_ref[pl.ds(kind, peers, stride=kinds), :]) for kind in range(kinds)],
        axis=0,
    )
    index = [ref[group : group + 1, :] for ref in (first_ref, second_ref) for group in range(groups)]
    step = 256
    block = lax.broadcasted_iota(jnp.int32, (step, lanes), 0)
    index = [jnp.broadcast_to(numbers, (step, lanes)).astype(jnp.int16) for numbers in index]
    for start in range(0, blocks, step):
        marks = jnp.concatenate(
            [ones_where((block + start).astype(jnp.int16) == numbers) for numbers in index], axis=1
        )
        product = jnp.dot(marks, rows, preferred_element_type=jnp.float32)
        part = slice(start, start + step)
        out_ref[part, :] = halves_added(product) / orbit_factor(orbit_ref[part, :])


def add_up(first, second, rows, orbit):
    blocks, columns = orbit.shape
    count = rows.shape[0]
    return pl.pallas_call(
        add_up_kernel,
        out_shape=jax.ShapeDtypeStruct((blocks, columns), jnp.float32),
        in_specs=[IN_VMEM] * 4,
        out_specs=IN_VMEM,
        compiler_params=pltpu.CompilerParams(vmem_limit_bytes=16 * MIB),
        cost_estimate=pl.CostEstimate(
            flops=4 * count * blocks * columns,
            bytes_accessed=(count + 2 * blocks) * columns * 4,
            transcendentals=blocks * columns,
        ),
        name="add_up",
    )(first, second, rows, orbit)


def per_device(amplitudes, orbit_index, requests, targets):
    columns = amplitudes.shape[1]
    nx, ny, nz, nc = (lax.axis_size(a) for a in AXES)
    plane = nx * ny * nc
    slots = requests.shape[-1]
    asked = deal(requests.reshape(-1, slots).T, nz)
    asked = lax.all_to_all(asked, "z", split_axis=0, concat_axis=0, tiled=True)
    wanted = lax.all_to_all(
        asked.transpose(2, 1, 0), PLANE, split_axis=0, concat_axis=0, tiled=True
    )
    table, own, landing = own_rows(amplitudes, orbit_index, targets.reshape(-1, slots).T)
    outgoing, wanted_landing = serve(wanted, table, own)
    arrived = lax.all_to_all(
        outgoing.reshape(nz * plane, 2 * slots, columns),
        PEERS,
        split_axis=0,
        concat_axis=0,
        tiled=True,
    )
    return add_up(wanted_landing, landing, arrived.reshape(-1, columns), orbit_index)


def solution(mesh):
    groups, shards = mesh.devices.shape
    devices = mesh.devices.reshape(groups, 4, shards // 8, 2)
    split = P(AXES)
    return jax.shard_map(
        per_device,
        mesh=Mesh(devices, AXES),
        in_specs=(split, split, split, split),
        out_specs=split,
        check_vma=False,
    )
```

```python
import jax
import jax.numpy as jnp
from jax import lax
from jax.experimental import pallas as pl
from jax.experimental.pallas import tpu as pltpu
from jax.sharding import Mesh
from jax.sharding import PartitionSpec as P

AXES = ("x", "y", "z", "c")
PEERS = ("z", "c", "x", "y")
PLANE = ("c", "x", "y")
IN_VMEM = pl.BlockSpec(memory_space=pltpu.VMEM)
MIB = 2**20
STEP = 8


def orbit_factor(orbit):
    return jnp.sqrt(96.0 * jnp.exp2(-orbit.astype(jnp.float32)))


def two_parts(values):
    high = values.astype(jnp.bfloat16)
    low = (values - high.astype(jnp.float32)).astype(jnp.bfloat16)
    return jnp.concatenate([high, low], axis=1)


def halves_added(product):
    columns = product.shape[1] // 2
    return product[:, :columns] + product[:, columns:]


def ones_where(hit):
    return jnp.where(hit, jnp.bfloat16(1.0), jnp.bfloat16(0.0))


def lanes_joined(pieces, lanes):
    share = lanes // pieces[0].shape[1]
    rows = [
        jnp.concatenate(pieces[start : start + share], axis=1)
        for start in range(0, len(pieces), share)
    ]
    return jnp.concatenate(rows, axis=0)


def deal_kernel(asked_ref, out_ref):
    slots, total = asked_ref.shape
    lines, _, width = out_ref.shape
    run = 32
    for slot in range(slots):
        grid = jnp.concatenate(
            [asked_ref[slot : slot + 1, start : start + run] for start in range(0, total, run)],
            axis=0,
        )
        turned = grid.T
        cores = run // lines
        for line in range(lines):
            out_ref[line, slot : slot + 1, :] = jnp.concatenate(
                [turned[line * cores + core : line * cores + core + 1, :] for core in range(cores)],
                axis=1,
            )


def deal(asked, lines):
    slots, total = asked.shape
    return pl.pallas_call(
        deal_kernel,
        out_shape=jax.ShapeDtypeStruct((lines, slots, total // lines), jnp.int32),
        in_specs=[IN_VMEM],
        out_specs=IN_VMEM,
        compiler_params=pltpu.CompilerParams(vmem_limit_bytes=4 * MIB),
        cost_estimate=pl.CostEstimate(flops=40960, bytes_accessed=40960, transcendentals=0),
        name="deal",
    )(asked)


def picked(columns, table, step):
    width = columns[0].shape[0]
    blocks = table.shape[0]
    block = lax.broadcasted_iota(jnp.int32, (width, blocks), 1).astype(jnp.int16)
    for first in range(0, len(columns), step):
        chosen = [ones_where(column.astype(jnp.int16) == block) for column in columns[first : first + step]]
        product = jnp.dot(
            jnp.concatenate(chosen, axis=0), table, preferred_element_type=jnp.float32
        )
        yield first * width, halves_added(product)


def own_kernel(weighted_ref, places_ref, table_ref, own_ref, landing_ref):
    table_ref[...] = two_parts(weighted_ref[...])
    slots, total = places_ref.shape
    run = 32
    lanes = landing_ref.shape[1]
    columns = []
    for slot in range(slots):
        grid = jnp.concatenate(
            [places_ref[slot : slot + 1, start : start + run] for start in range(0, total, run)],
            axis=0,
        )
        columns += [grid[:, column : column + 1] for column in range(run)]
        turned = grid.T
        share = total // lanes
        landing_ref[slot * share : (slot + 1) * share, :] = lanes_joined(
            [turned[row : row + 1, :] for row in range(run)], lanes
        )
    for first, rows in picked(columns, table_ref[...], 16):
        own_ref[first : first + rows.shape[0], :] = rows


def own_rows(weighted, places):
    blocks, columns = weighted.shape
    rows = places.size
    return pl.pallas_call(
        own_kernel,
        out_shape=(
            jax.ShapeDtypeStruct((blocks, 2 * columns), jnp.bfloat16),
            jax.ShapeDtypeStruct((rows, columns), jnp.float32),
            jax.ShapeDtypeStruct((rows // 128, 128), jnp.int32),
        ),
        in_specs=[IN_VMEM] * 2,
        out_specs=(IN_VMEM,) * 3,
        compiler_params=pltpu.CompilerParams(vmem_limit_bytes=16 * MIB),
        cost_estimate=pl.CostEstimate(
            flops=rows * columns,
            bytes_accessed=rows * columns,
            transcendentals=0,
        ),
        name="own_rows",
    )(weighted, places)


def serve_kernel(wanted_ref, table_ref, own_ref, out_ref, landing_ref):
    width, slots, lines = wanted_ref.shape
    lanes = landing_ref.shape[1]
    peers = lines * width
    share = peers // lanes
    for slot in range(slots):
        part = slice(slot * peers, (slot + 1) * peers)
        out_ref[pl.ds(slot, peers, stride=2 * slots), :] = own_ref[part, :]
    whole = jnp.concatenate([wanted_ref[:, slot, :] for slot in range(slots)], axis=1)
    square = whole.T
    numbers = [square[slot * lines : (slot + 1) * lines, :] for slot in range(slots)]
    turned = [whole[:, slot * lines : (slot + 1) * lines] for slot in range(slots)]
    columns = [turn[:, line : line + 1] for turn in turned for line in range(lines)]
    for first, rows in picked(columns, table_ref[...], 8):
        slot, start = divmod(first, peers)
        out_ref[
            pl.ds(start * 2 * slots + slots + slot, rows.shape[0], stride=2 * slots), :
        ] = rows
    for slot in range(slots):
        landing_ref[slot * share : (slot + 1) * share, :] = lanes_joined(
            [numbers[slot][line : line + 1, :] for line in range(lines)], lanes
        )


def serve(wanted, table, own):
    rows, columns = own.shape
    blocks = table.shape[0]
    return pl.pallas_call(
        serve_kernel,
        out_shape=(
            jax.ShapeDtypeStruct((2 * rows, columns), jnp.float32),
            jax.ShapeDtypeStruct((rows // 128, 128), jnp.int32),
        ),
        in_specs=[IN_VMEM] * 3,
        out_specs=(IN_VMEM,) * 2,
        compiler_params=pltpu.CompilerParams(vmem_limit_bytes=16 * MIB),
        cost_estimate=pl.CostEstimate(
            flops=4 * rows * blocks * columns,
            bytes_accessed=16 * rows * columns,
            transcendentals=0,
        ),
        name="serve",
    )(wanted, table, own)


def add_up_kernel(first_ref, second_ref, rows_ref, orbit_ref, out_ref):
    groups, lanes = first_ref.shape
    blocks = out_ref.shape[0]
    count = rows_ref.shape[0]
    peers = groups * lanes // 2
    kinds = count // peers
    rows = jnp.concatenate(
        [two_parts(rows_ref[pl.ds(kind, peers, stride=kinds), :]) for kind in range(kinds)],
        axis=0,
    )
    index = [ref[group : group + 1, :] for ref in (first_ref, second_ref) for group in range(groups)]
    step = 256
    block = lax.broadcasted_iota(jnp.int32, (step, lanes), 0)
    index = [jnp.broadcast_to(numbers, (step, lanes)).astype(jnp.int16) for numbers in index]
    for start in range(0, blocks, step):
        marks = jnp.concatenate(
            [ones_where((block + start).astype(jnp.int16) == numbers) for numbers in index], axis=1
        )
        product = jnp.dot(marks, rows, preferred_element_type=jnp.float32)
        part = slice(start, start + step)
        out_ref[part, :] = halves_added(product) / orbit_factor(orbit_ref[part, :])


def add_up(first, second, rows, orbit):
    blocks, columns = orbit.shape
    count = rows.shape[0]
    return pl.pallas_call(
        add_up_kernel,
        out_shape=jax.ShapeDtypeStruct((blocks, columns), jnp.float32),
        in_specs=[IN_VMEM] * 4,
        out_specs=IN_VMEM,
        compiler_params=pltpu.CompilerParams(vmem_limit_bytes=16 * MIB),
        cost_estimate=pl.CostEstimate(
            flops=4 * count * blocks * columns,
            bytes_accessed=(count + 2 * blocks) * columns * 4,
            transcendentals=blocks * columns,
        ),
        name="add_up",
    )(first, second, rows, orbit)


def per_device(amplitudes, orbit_index, requests, targets):
    columns = amplitudes.shape[1]
    nx, ny, nz, nc = (lax.axis_size(a) for a in AXES)
    plane = nx * ny * nc
    slots = requests.shape[-1]
    asked = deal(requests.reshape(-1, slots).T, nz)
    asked = lax.all_to_all(asked, "z", split_axis=0, concat_axis=0, tiled=True)
    wanted = lax.all_to_all(
        asked.transpose(2, 1, 0), PLANE, split_axis=0, concat_axis=0, tiled=True
    )
    weighted = amplitudes * orbit_factor(orbit_index)
    table, own, landing = own_rows(weighted, targets.reshape(-1, slots).T)
    outgoing, wanted_landing = serve(wanted, table, own)
    arrived = lax.all_to_all(
        outgoing.reshape(nz * plane, 2 * slots, columns),
        PEERS,
        split_axis=0,
        concat_axis=0,
        tiled=True,
    )
    return add_up(wanted_landing, landing, arrived.reshape(-1, columns), orbit_index)


def solution(mesh):
    groups, shards = mesh.devices.shape
    devices = mesh.devices.reshape(groups, 4, shards // 8, 2)
    split = P(AXES)
    return jax.shard_map(
        per_device,
        mesh=Mesh(devices, AXES),
        in_specs=(split, split, split, split),
        out_specs=split,
        check_vma=False,
    )
```

```python
import jax
import jax.numpy as jnp
from jax import lax
from jax.experimental import pallas as pl
from jax.experimental.pallas import tpu as pltpu
from jax.sharding import Mesh
from jax.sharding import PartitionSpec as P

AXES = ("x", "y", "z", "c")
PEERS = ("z", "c", "x", "y")
PLANE = ("c", "x", "y")
IN_VMEM = pl.BlockSpec(memory_space=pltpu.VMEM)
MIB = 2**20
STEP = 8


def orbit_factor(orbit):
    return jnp.sqrt(96.0 * jnp.exp2(-orbit.astype(jnp.float32)))


def two_parts(values):
    high = values.astype(jnp.bfloat16)
    low = (values - high.astype(jnp.float32)).astype(jnp.bfloat16)
    return jnp.concatenate([high, low], axis=1)


def halves_added(product):
    columns = product.shape[1] // 2
    return product[:, :columns] + product[:, columns:]


def ones_where(hit):
    return jnp.where(hit, jnp.bfloat16(1.0), jnp.bfloat16(0.0))


def lanes_joined(pieces, lanes):
    share = lanes // pieces[0].shape[1]
    rows = [
        jnp.concatenate(pieces[start : start + share], axis=1)
        for start in range(0, len(pieces), share)
    ]
    return jnp.concatenate(rows, axis=0)


def deal_kernel(asked_ref, out_ref):
    slots, total = asked_ref.shape
    lines, _, width = out_ref.shape
    run = 32
    for slot in range(slots):
        grid = jnp.concatenate(
            [asked_ref[slot : slot + 1, start : start + run] for start in range(0, total, run)],
            axis=0,
        )
        turned = grid.T
        cores = run // lines
        for line in range(lines):
            out_ref[line, slot : slot + 1, :] = jnp.concatenate(
                [turned[line * cores + core : line * cores + core + 1, :] for core in range(cores)],
                axis=1,
            )


def deal(asked, lines):
    slots, total = asked.shape
    return pl.pallas_call(
        deal_kernel,
        out_shape=jax.ShapeDtypeStruct((lines, slots, total // lines), jnp.int32),
        in_specs=[IN_VMEM],
        out_specs=IN_VMEM,
        compiler_params=pltpu.CompilerParams(vmem_limit_bytes=4 * MIB),
        cost_estimate=pl.CostEstimate(flops=40960, bytes_accessed=40960, transcendentals=0),
        name="deal",
    )(asked)


def picked(columns, table, step):
    width = columns[0].shape[0]
    blocks = table.shape[0]
    block = lax.broadcasted_iota(jnp.int32, (width, blocks), 1).astype(jnp.int16)
    for first in range(0, len(columns), step):
        chosen = [ones_where(column.astype(jnp.int16) == block) for column in columns[first : first + step]]
        product = jnp.dot(
            jnp.concatenate(chosen, axis=0), table, preferred_element_type=jnp.float32
        )
        yield first * width, halves_added(product)


def own_kernel(amplitudes_ref, orbit_ref, places_ref, table_ref, own_ref, landing_ref):
    table_ref[...] = two_parts(amplitudes_ref[...] * orbit_factor(orbit_ref[...]))
    slots, total = places_ref.shape
    run = 32
    lanes = landing_ref.shape[1]
    columns = []
    for slot in range(slots):
        grid = jnp.concatenate(
            [places_ref[slot : slot + 1, start : start + run] for start in range(0, total, run)],
            axis=0,
        )
        columns += [grid[:, column : column + 1] for column in range(run)]
        turned = grid.T
        share = total // lanes
        landing_ref[slot * share : (slot + 1) * share, :] = lanes_joined(
            [turned[row : row + 1, :] for row in range(run)], lanes
        )
    for first, rows in picked(columns, table_ref[...], 16):
        own_ref[first : first + rows.shape[0], :] = rows


def own_rows(amplitudes, orbit, places):
    blocks, columns = amplitudes.shape
    rows = places.size
    return pl.pallas_call(
        own_kernel,
        out_shape=(
            jax.ShapeDtypeStruct((blocks, 2 * columns), jnp.bfloat16),
            jax.ShapeDtypeStruct((rows, columns), jnp.float32),
            jax.ShapeDtypeStruct((rows // 128, 128), jnp.int32),
        ),
        in_specs=[IN_VMEM] * 3,
        out_specs=(IN_VMEM,) * 3,
        compiler_params=pltpu.CompilerParams(vmem_limit_bytes=16 * MIB),
        cost_estimate=pl.CostEstimate(
            flops=4 * rows * blocks * columns,
            bytes_accessed=20 * blocks * columns,
            transcendentals=blocks * columns,
        ),
        name="own_rows",
    )(amplitudes, orbit, places)


def serve_kernel(wanted_ref, table_ref, own_ref, out_ref, landing_ref):
    width, slots, lines = wanted_ref.shape
    lanes = landing_ref.shape[1]
    peers = lines * width
    share = peers // lanes
    for slot in range(slots):
        part = slice(slot * peers, (slot + 1) * peers)
        out_ref[pl.ds(slot, peers, stride=2 * slots), :] = own_ref[part, :]
    whole = jnp.concatenate([wanted_ref[:, slot, :] for slot in range(slots)], axis=1)
    square = whole.T
    numbers = [square[slot * lines : (slot + 1) * lines, :] for slot in range(slots)]
    turned = [whole[:, slot * lines : (slot + 1) * lines] for slot in range(slots)]
    columns = [turn[:, line : line + 1] for turn in turned for line in range(lines)]
    for first, rows in picked(columns, table_ref[...], 8):
        slot, start = divmod(first, peers)
        out_ref[
            pl.ds(start * 2 * slots + slots + slot, rows.shape[0], stride=2 * slots), :
        ] = rows
    for slot in range(slots):
        landing_ref[slot * share : (slot + 1) * share, :] = lanes_joined(
            [numbers[slot][line : line + 1, :] for line in range(lines)], lanes
        )


def serve(wanted, table, own):
    rows, columns = own.shape
    blocks = table.shape[0]
    return pl.pallas_call(
        serve_kernel,
        out_shape=(
            jax.ShapeDtypeStruct((2 * rows, columns), jnp.float32),
            jax.ShapeDtypeStruct((rows // 128, 128), jnp.int32),
        ),
        in_specs=[IN_VMEM] * 3,
        out_specs=(IN_VMEM,) * 2,
        compiler_params=pltpu.CompilerParams(vmem_limit_bytes=16 * MIB),
        cost_estimate=pl.CostEstimate(
            flops=4 * rows * blocks * columns,
            bytes_accessed=16 * rows * columns,
            transcendentals=0,
        ),
        name="serve",
    )(wanted, table, own)


def add_up_kernel(first_ref, second_ref, rows_ref, orbit_ref, out_ref, held_ref, sent):
    groups, lanes = first_ref.shape
    blocks = out_ref.shape[0]
    count = rows_ref.shape[0]
    peers = groups * lanes // 2
    kinds = count // peers
    share = peers // lanes
    index = [ref[group : group + 1, :] for ref in (first_ref, second_ref) for group in range(groups)]
    step = 256
    block = lax.broadcasted_iota(jnp.int32, (step, lanes), 0)
    index = [jnp.broadcast_to(numbers, (step, lanes)).astype(jnp.int16) for numbers in index]
    parts = {}
    copies = []
    for start in range(0, blocks, step):
        here = (block + start).astype(jnp.int16)
        total = None
        for kind in range(kinds):
            if kind not in parts:
                parts[kind] = two_parts(rows_ref[pl.ds(kind, peers, stride=kinds), :])
            marks = jnp.concatenate(
                [ones_where(here == numbers) for numbers in index[kind * share : (kind + 1) * share]], axis=1
            )
            product = jnp.dot(marks, parts[kind], preferred_element_type=jnp.float32)
            total = product if total is None else total + product
        part = slice(start, start + step)
        held_ref[part, :] = halves_added(total) / orbit_factor(orbit_ref[part, :])
        copy = pltpu.make_async_copy(held_ref.at[part, :], out_ref.at[part, :], sent.at[start // step])
        copy.start()
        copies.append(copy)
    for copy in copies:
        copy.wait()


def add_up(first, second, rows, orbit):
    blocks, columns = orbit.shape
    count = rows.shape[0]
    return pl.pallas_call(
        add_up_kernel,
        out_shape=jax.ShapeDtypeStruct((blocks, columns), jnp.float32),
        in_specs=[IN_VMEM] * 4,
        out_specs=pl.BlockSpec(memory_space=pl.ANY),
        scratch_shapes=[
            pltpu.VMEM((blocks, columns), jnp.float32),
            pltpu.SemaphoreType.DMA((blocks // 256,)),
        ],
        compiler_params=pltpu.CompilerParams(vmem_limit_bytes=16 * MIB),
        cost_estimate=pl.CostEstimate(
            flops=4 * count * blocks * columns,
            bytes_accessed=(count + 2 * blocks) * columns * 4,
            transcendentals=blocks * columns,
        ),
        name="add_up",
    )(first, second, rows, orbit)


def per_device(amplitudes, orbit_index, requests, targets):
    columns = amplitudes.shape[1]
    nx, ny, nz, nc = (lax.axis_size(a) for a in AXES)
    plane = nx * ny * nc
    slots = requests.shape[-1]
    asked = deal(requests.reshape(-1, slots).T, nz)
    asked = lax.all_to_all(asked, "z", split_axis=0, concat_axis=0, tiled=True)
    wanted = lax.all_to_all(
        asked.transpose(2, 1, 0), PLANE, split_axis=0, concat_axis=0, tiled=True
    )
    table, own, landing = own_rows(amplitudes, orbit_index, targets.reshape(-1, slots).T)
    outgoing, wanted_landing = serve(wanted, table, own)
    arrived = lax.all_to_all(
        outgoing.reshape(nz * plane, 2 * slots, columns),
        PEERS,
        split_axis=0,
        concat_axis=0,
        tiled=True,
    )
    return add_up(wanted_landing, landing, arrived.reshape(-1, columns), orbit_index)


def solution(mesh):
    groups, shards = mesh.devices.shape
    devices = mesh.devices.reshape(groups, 4, shards // 8, 2)
    split = P(AXES)
    return jax.shard_map(
        per_device,
        mesh=Mesh(devices, AXES),
        in_specs=(split, split, split, split),
        out_specs=split,
        check_vma=False,
    )
```

```python
import jax
import jax.numpy as jnp
from jax import lax
from jax.experimental import pallas as pl
from jax.experimental.pallas import tpu as pltpu
from jax.sharding import Mesh
from jax.sharding import PartitionSpec as P

AXES = ("x", "y", "z", "c")
PEERS = ("z", "c", "x", "y")
PLANE = ("c", "x", "y")
IN_VMEM = pl.BlockSpec(memory_space=pltpu.VMEM)
MIB = 2**20
STEP = 8


def orbit_factor(orbit):
    return jnp.sqrt(96.0 * jnp.exp2(-orbit.astype(jnp.float32)))


def two_parts(values):
    high = values.astype(jnp.bfloat16)
    low = (values - high.astype(jnp.float32)).astype(jnp.bfloat16)
    return jnp.concatenate([high, low], axis=1)


def halves_added(product):
    columns = product.shape[1] // 2
    return product[:, :columns] + product[:, columns:]


def ones_where(hit):
    return jnp.where(hit, jnp.bfloat16(1.0), jnp.bfloat16(0.0))


def lanes_joined(pieces, lanes):
    share = lanes // pieces[0].shape[1]
    rows = [
        jnp.concatenate(pieces[start : start + share], axis=1)
        for start in range(0, len(pieces), share)
    ]
    return jnp.concatenate(rows, axis=0)


def deal_kernel(asked_ref, out_ref):
    slots, total = asked_ref.shape
    lines, _, width = out_ref.shape
    run = 32
    for slot in range(slots):
        grid = jnp.concatenate(
            [asked_ref[slot : slot + 1, start : start + run] for start in range(0, total, run)],
            axis=0,
        )
        turned = grid.T
        cores = run // lines
        for line in range(lines):
            out_ref[line, slot : slot + 1, :] = jnp.concatenate(
                [turned[line * cores + core : line * cores + core + 1, :] for core in range(cores)],
                axis=1,
            )


def deal(asked, lines):
    slots, total = asked.shape
    return pl.pallas_call(
        deal_kernel,
        out_shape=jax.ShapeDtypeStruct((lines, slots, total // lines), jnp.int32),
        in_specs=[IN_VMEM],
        out_specs=IN_VMEM,
        compiler_params=pltpu.CompilerParams(vmem_limit_bytes=4 * MIB),
        cost_estimate=pl.CostEstimate(flops=40960, bytes_accessed=40960, transcendentals=0),
        name="deal",
    )(asked)


def picked(columns, table, step):
    width = columns[0].shape[0]
    blocks = table.shape[0]
    block = lax.broadcasted_iota(jnp.int32, (width, blocks), 1).astype(jnp.int16)
    for first in range(0, len(columns), step):
        chosen = [ones_where(column.astype(jnp.int16) == block) for column in columns[first : first + step]]
        product = jnp.dot(
            jnp.concatenate(chosen, axis=0), table, preferred_element_type=jnp.float32
        )
        yield first * width, halves_added(product)


def own_kernel(weighted_ref, places_ref, table_ref, own_ref, landing_ref):
    table_ref[...] = two_parts(weighted_ref[...])
    slots, total = places_ref.shape
    run = 32
    lanes = landing_ref.shape[1]
    columns = []
    for slot in range(slots):
        grid = jnp.concatenate(
            [places_ref[slot : slot + 1, start : start + run] for start in range(0, total, run)],
            axis=0,
        )
        columns += [grid[:, column : column + 1] for column in range(run)]
        turned = grid.T
        share = total // lanes
        landing_ref[slot * share : (slot + 1) * share, :] = lanes_joined(
            [turned[row : row + 1, :] for row in range(run)], lanes
        )
    for first, rows in picked(columns, table_ref[...], 16):
        own_ref[first : first + rows.shape[0], :] = rows


def own_rows(weighted, places):
    blocks, columns = weighted.shape
    rows = places.size
    return pl.pallas_call(
        own_kernel,
        out_shape=(
            jax.ShapeDtypeStruct((blocks, 2 * columns), jnp.bfloat16),
            jax.ShapeDtypeStruct((rows, columns), jnp.float32),
            jax.ShapeDtypeStruct((rows // 128, 128), jnp.int32),
        ),
        in_specs=[IN_VMEM] * 2,
        out_specs=(IN_VMEM,) * 3,
        compiler_params=pltpu.CompilerParams(vmem_limit_bytes=16 * MIB),
        cost_estimate=pl.CostEstimate(
            flops=rows * columns,
            bytes_accessed=rows * columns,
            transcendentals=0,
        ),
        name="own_rows",
    )(weighted, places)


def serve_kernel(wanted_ref, table_ref, own_ref, out_ref, landing_ref):
    width, slots, lines = wanted_ref.shape
    lanes = landing_ref.shape[1]
    peers = lines * width
    share = peers // lanes
    for slot in range(slots):
        part = slice(slot * peers, (slot + 1) * peers)
        out_ref[pl.ds(slot, peers, stride=2 * slots), :] = own_ref[part, :]
    whole = jnp.concatenate([wanted_ref[:, slot, :] for slot in range(slots)], axis=1)
    square = whole.T
    numbers = [square[slot * lines : (slot + 1) * lines, :] for slot in range(slots)]
    turned = [whole[:, slot * lines : (slot + 1) * lines] for slot in range(slots)]
    columns = [turn[:, line : line + 1] for turn in turned for line in range(lines)]
    for first, rows in picked(columns, table_ref[...], 8):
        slot, start = divmod(first, peers)
        out_ref[
            pl.ds(start * 2 * slots + slots + slot, rows.shape[0], stride=2 * slots), :
        ] = rows
    for slot in range(slots):
        landing_ref[slot * share : (slot + 1) * share, :] = lanes_joined(
            [numbers[slot][line : line + 1, :] for line in range(lines)], lanes
        )


def serve(wanted, table, own):
    rows, columns = own.shape
    blocks = table.shape[0]
    return pl.pallas_call(
        serve_kernel,
        out_shape=(
            jax.ShapeDtypeStruct((2 * rows, columns), jnp.float32),
            jax.ShapeDtypeStruct((rows // 128, 128), jnp.int32),
        ),
        in_specs=[IN_VMEM] * 3,
        out_specs=(IN_VMEM,) * 2,
        compiler_params=pltpu.CompilerParams(vmem_limit_bytes=16 * MIB),
        cost_estimate=pl.CostEstimate(
            flops=4 * rows * blocks * columns,
            bytes_accessed=16 * rows * columns,
            transcendentals=0,
        ),
        name="serve",
    )(wanted, table, own)


def add_up_kernel(first_ref, second_ref, rows_ref, orbit_ref, out_ref, held_ref, sent):
    groups, lanes = first_ref.shape
    blocks = out_ref.shape[0]
    count = rows_ref.shape[0]
    peers = groups * lanes // 2
    kinds = count // peers
    share = peers // lanes
    index = [ref[group : group + 1, :] for ref in (first_ref, second_ref) for group in range(groups)]
    step = 256
    block = lax.broadcasted_iota(jnp.int32, (step, lanes), 0)
    index = [jnp.broadcast_to(numbers, (step, lanes)).astype(jnp.int16) for numbers in index]
    parts = {}
    copies = []
    for start in range(0, blocks, step):
        here = (block + start).astype(jnp.int16)
        total = None
        for kind in range(kinds):
            if kind not in parts:
                parts[kind] = two_parts(rows_ref[pl.ds(kind, peers, stride=kinds), :])
            marks = jnp.concatenate(
                [ones_where(here == numbers) for numbers in index[kind * share : (kind + 1) * share]], axis=1
            )
            product = jnp.dot(marks, parts[kind], preferred_element_type=jnp.float32)
            total = product if total is None else total + product
        part = slice(start, start + step)
        held_ref[part, :] = halves_added(total) / orbit_factor(orbit_ref[part, :])
        copy = pltpu.make_async_copy(held_ref.at[part, :], out_ref.at[part, :], sent.at[start // step])
        copy.start()
        copies.append(copy)
    for copy in copies:
        copy.wait()


def add_up(first, second, rows, orbit):
    blocks, columns = orbit.shape
    count = rows.shape[0]
    return pl.pallas_call(
        add_up_kernel,
        out_shape=jax.ShapeDtypeStruct((blocks, columns), jnp.float32),
        in_specs=[IN_VMEM] * 4,
        out_specs=pl.BlockSpec(memory_space=pl.ANY),
        scratch_shapes=[
            pltpu.VMEM((blocks, columns), jnp.float32),
            pltpu.SemaphoreType.DMA((blocks // 256,)),
        ],
        compiler_params=pltpu.CompilerParams(vmem_limit_bytes=16 * MIB),
        cost_estimate=pl.CostEstimate(
            flops=4 * count * blocks * columns,
            bytes_accessed=(count + 2 * blocks) * columns * 4,
            transcendentals=blocks * columns,
        ),
        name="add_up",
    )(first, second, rows, orbit)


def per_device(amplitudes, orbit_index, requests, targets):
    columns = amplitudes.shape[1]
    nx, ny, nz, nc = (lax.axis_size(a) for a in AXES)
    plane = nx * ny * nc
    slots = requests.shape[-1]
    asked = deal(requests.reshape(-1, slots).T, nz)
    asked = lax.all_to_all(asked, "z", split_axis=0, concat_axis=0, tiled=True)
    wanted = lax.all_to_all(
        asked.transpose(2, 1, 0), PLANE, split_axis=0, concat_axis=0, tiled=True
    )
    weighted = amplitudes * orbit_factor(orbit_index)
    table, own, landing = own_rows(weighted, targets.reshape(-1, slots).T)
    outgoing, wanted_landing = serve(wanted, table, own)
    arrived = lax.all_to_all(
        outgoing.reshape(nz * plane, 2 * slots, columns),
        PEERS,
        split_axis=0,
        concat_axis=0,
        tiled=True,
    )
    return add_up(wanted_landing, landing, arrived.reshape(-1, columns), orbit_index)


def solution(mesh):
    groups, shards = mesh.devices.shape
    devices = mesh.devices.reshape(groups, 4, shards // 8, 2)
    split = P(AXES)
    return jax.shard_map(
        per_device,
        mesh=Mesh(devices, AXES),
        in_specs=(split, split, split, split),
        out_specs=split,
        check_vma=False,
    )
```

```python
import jax
import jax.numpy as jnp
from jax import lax
from jax.experimental import pallas as pl
from jax.experimental.pallas import tpu as pltpu
from jax.sharding import Mesh
from jax.sharding import PartitionSpec as P

AXES = ("x", "y", "z", "c")
PEERS = ("z", "c", "x", "y")
PLANE = ("c", "x", "y")
IN_VMEM = pl.BlockSpec(memory_space=pltpu.VMEM)
MIB = 2**20
STEP = 8


def orbit_factor(orbit):
    return jnp.sqrt(96.0 * jnp.exp2(-orbit.astype(jnp.float32)))


def two_parts(values):
    high = values.astype(jnp.bfloat16)
    low = (values - high.astype(jnp.float32)).astype(jnp.bfloat16)
    return jnp.concatenate([high, low], axis=1)


def halves_added(product):
    columns = product.shape[1] // 2
    return product[:, :columns] + product[:, columns:]


def ones_where(hit):
    return jnp.where(hit, jnp.bfloat16(1.0), jnp.bfloat16(0.0))


def lanes_joined(pieces, lanes):
    share = lanes // pieces[0].shape[1]
    rows = [
        jnp.concatenate(pieces[start : start + share], axis=1)
        for start in range(0, len(pieces), share)
    ]
    return jnp.concatenate(rows, axis=0)


def deal_kernel(asked_ref, out_ref):
    slots, total = asked_ref.shape
    lines, _, width = out_ref.shape
    run = 32
    for slot in range(slots):
        grid = jnp.concatenate(
            [asked_ref[slot : slot + 1, start : start + run] for start in range(0, total, run)],
            axis=0,
        )
        turned = grid.T
        cores = run // lines
        for line in range(lines):
            out_ref[line, slot : slot + 1, :] = jnp.concatenate(
                [turned[line * cores + core : line * cores + core + 1, :] for core in range(cores)],
                axis=1,
            )


def deal(asked, lines):
    slots, total = asked.shape
    return pl.pallas_call(
        deal_kernel,
        out_shape=jax.ShapeDtypeStruct((lines, slots, total // lines), jnp.int32),
        in_specs=[IN_VMEM],
        out_specs=IN_VMEM,
        compiler_params=pltpu.CompilerParams(vmem_limit_bytes=4 * MIB),
        cost_estimate=pl.CostEstimate(flops=40960, bytes_accessed=40960, transcendentals=0),
        name="deal",
    )(asked)


def picked(columns, table, step):
    width = columns[0].shape[0]
    blocks = table.shape[0]
    block = lax.broadcasted_iota(jnp.int32, (width, blocks), 1).astype(jnp.int16)
    for first in range(0, len(columns), step):
        chosen = [ones_where(column.astype(jnp.int16) == block) for column in columns[first : first + step]]
        product = jnp.dot(
            jnp.concatenate(chosen, axis=0), table, preferred_element_type=jnp.float32
        )
        yield first * width, halves_added(product)


def own_kernel(amplitudes_ref, orbit_ref, places_ref, table_ref, own_ref, landing_ref):
    table_ref[...] = two_parts(amplitudes_ref[...] * orbit_factor(orbit_ref[...]))
    slots, total = places_ref.shape
    run = 32
    lanes = landing_ref.shape[1]
    columns = []
    for slot in range(slots):
        grid = jnp.concatenate(
            [places_ref[slot : slot + 1, start : start + run] for start in range(0, total, run)],
            axis=0,
        )
        columns += [grid[:, column : column + 1] for column in range(run)]
        turned = grid.T
        share = total // lanes
        landing_ref[slot * share : (slot + 1) * share, :] = lanes_joined(
            [turned[row : row + 1, :] for row in range(run)], lanes
        )
    for first, rows in picked(columns, table_ref[...], 16):
        own_ref[first : first + rows.shape[0], :] = rows


def own_rows(amplitudes, orbit, places):
    blocks, columns = amplitudes.shape
    rows = places.size
    return pl.pallas_call(
        own_kernel,
        out_shape=(
            jax.ShapeDtypeStruct((blocks, 2 * columns), jnp.bfloat16),
            jax.ShapeDtypeStruct((rows, columns), jnp.float32),
            jax.ShapeDtypeStruct((rows // 128, 128), jnp.int32),
        ),
        in_specs=[IN_VMEM] * 3,
        out_specs=(IN_VMEM,) * 3,
        compiler_params=pltpu.CompilerParams(vmem_limit_bytes=16 * MIB),
        cost_estimate=pl.CostEstimate(
            flops=4 * rows * blocks * columns,
            bytes_accessed=20 * blocks * columns,
            transcendentals=blocks * columns,
        ),
        name="own_rows",
    )(amplitudes, orbit, places)


def serve_kernel(wanted_ref, table_ref, own_ref, out_ref, landing_ref):
    width, slots, lines = wanted_ref.shape
    lanes = landing_ref.shape[1]
    peers = lines * width
    share = peers // lanes
    for slot in range(slots):
        part = slice(slot * peers, (slot + 1) * peers)
        out_ref[pl.ds(slot, peers, stride=2 * slots), :] = own_ref[part, :]
    whole = jnp.concatenate([wanted_ref[:, slot, :] for slot in range(slots)], axis=1)
    square = whole.T
    numbers = [square[slot * lines : (slot + 1) * lines, :] for slot in range(slots)]
    turned = [whole[:, slot * lines : (slot + 1) * lines] for slot in range(slots)]
    columns = [turn[:, line : line + 1] for turn in turned for line in range(lines)]
    for first, rows in picked(columns, table_ref[...], 16):
        slot, start = divmod(first, peers)
        out_ref[
            pl.ds(start * 2 * slots + slots + slot, rows.shape[0], stride=2 * slots), :
        ] = rows
    for slot in range(slots):
        landing_ref[slot * share : (slot + 1) * share, :] = lanes_joined(
            [numbers[slot][line : line + 1, :] for line in range(lines)], lanes
        )


def serve(wanted, table, own):
    rows, columns = own.shape
    blocks = table.shape[0]
    return pl.pallas_call(
        serve_kernel,
        out_shape=(
            jax.ShapeDtypeStruct((2 * rows, columns), jnp.float32),
            jax.ShapeDtypeStruct((rows // 128, 128), jnp.int32),
        ),
        in_specs=[IN_VMEM] * 3,
        out_specs=(IN_VMEM,) * 2,
        compiler_params=pltpu.CompilerParams(vmem_limit_bytes=16 * MIB),
        cost_estimate=pl.CostEstimate(
            flops=4 * rows * blocks * columns,
            bytes_accessed=16 * rows * columns,
            transcendentals=0,
        ),
        name="serve",
    )(wanted, table, own)


def add_up_kernel(first_ref, second_ref, rows_ref, orbit_ref, out_ref, held_ref, sent):
    groups, lanes = first_ref.shape
    blocks = out_ref.shape[0]
    count = rows_ref.shape[0]
    peers = groups * lanes // 2
    kinds = count // peers
    share = peers // lanes
    index = [ref[group : group + 1, :] for ref in (first_ref, second_ref) for group in range(groups)]
    step = 256
    block = lax.broadcasted_iota(jnp.int32, (step, lanes), 0)
    index = [jnp.broadcast_to(numbers, (step, lanes)).astype(jnp.int16) for numbers in index]
    parts = {}
    copies = []
    for start in range(0, blocks, step):
        here = (block + start).astype(jnp.int16)
        total = None
        for kind in range(kinds):
            if kind not in parts:
                parts[kind] = two_parts(rows_ref[pl.ds(kind, peers, stride=kinds), :])
            marks = jnp.concatenate(
                [ones_where(here == numbers) for numbers in index[kind * share : (kind + 1) * share]], axis=1
            )
            product = jnp.dot(marks, parts[kind], preferred_element_type=jnp.float32)
            total = product if total is None else total + product
        part = slice(start, start + step)
        held_ref[part, :] = halves_added(total) / orbit_factor(orbit_ref[part, :])
        copy = pltpu.make_async_copy(held_ref.at[part, :], out_ref.at[part, :], sent.at[start // step])
        copy.start()
        copies.append(copy)
    for copy in copies:
        copy.wait()


def add_up(first, second, rows, orbit):
    blocks, columns = orbit.shape
    count = rows.shape[0]
    return pl.pallas_call(
        add_up_kernel,
        out_shape=jax.ShapeDtypeStruct((blocks, columns), jnp.float32),
        in_specs=[IN_VMEM] * 4,
        out_specs=pl.BlockSpec(memory_space=pl.ANY),
        scratch_shapes=[
            pltpu.VMEM((blocks, columns), jnp.float32),
            pltpu.SemaphoreType.DMA((blocks // 256,)),
        ],
        compiler_params=pltpu.CompilerParams(vmem_limit_bytes=16 * MIB),
        cost_estimate=pl.CostEstimate(
            flops=4 * count * blocks * columns,
            bytes_accessed=(count + 2 * blocks) * columns * 4,
            transcendentals=blocks * columns,
        ),
        name="add_up",
    )(first, second, rows, orbit)


def per_device(amplitudes, orbit_index, requests, targets):
    columns = amplitudes.shape[1]
    nx, ny, nz, nc = (lax.axis_size(a) for a in AXES)
    plane = nx * ny * nc
    slots = requests.shape[-1]
    asked = deal(requests.reshape(-1, slots).T, nz)
    asked = lax.all_to_all(asked, "z", split_axis=0, concat_axis=0, tiled=True)
    wanted = lax.all_to_all(
        asked.transpose(2, 1, 0), PLANE, split_axis=0, concat_axis=0, tiled=True
    )
    table, own, landing = own_rows(amplitudes, orbit_index, targets.reshape(-1, slots).T)
    outgoing, wanted_landing = serve(wanted, table, own)
    arrived = lax.all_to_all(
        outgoing.reshape(nz * plane, 2 * slots, columns),
        PEERS,
        split_axis=0,
        concat_axis=0,
        tiled=True,
    )
    return add_up(wanted_landing, landing, arrived.reshape(-1, columns), orbit_index)


def solution(mesh):
    groups, shards = mesh.devices.shape
    devices = mesh.devices.reshape(groups, 4, shards // 8, 2)
    split = P(AXES)
    return jax.shard_map(
        per_device,
        mesh=Mesh(devices, AXES),
        in_specs=(split, split, split, split),
        out_specs=split,
        check_vma=False,
    )
```
